32 devices in a mesh: outer: 8 (over y, x, core), bisect: 4 (over z).
Axes of the slice: x: 2, y: 2, z: 4, core: 2. Of those that a mesh axis runs over, the one named last changes fastest.
Arguments:
- positions: float32 [3, 32768], P(None, ('outer', 'bisect')), may hold values from -5 to 5, as said below
- masses: float32 [32768], P(('outer', 'bisect')), may hold values from 0.00048828125 to 0.0078125
- velocities: float32 [3, 32768], P(None, ('outer', 'bisect')), may hold values from -4 to 4
- essential: int32 [64, 4], P(('outer', 'bisect')), may hold values from 0 to 7, as said below
- list_count: int32 [64, 4], P('outer', 'bisect'), may hold values from 0 to 4, as said below
- list_target: int32 [64, 4, 4], P('outer', 'bisect'), may hold values from 0 to 7
- list_source: int32 [64, 4, 4], P('outer', 'bisect'), may hold values from 0 to 7
Outputs:
- new_positions: float32 [3, 32768], P(None, ('outer', 'bisect'))
- new_velocities: float32 [3, 32768], P(None, ('outer', 'bisect'))
The draws below stay inside these ranges and needn't reach their ends.
Inputs may be any that keep to these rules, and one draw needn't show every extreme that they name: `positions`: the volume spans -0.25 to 0.25 along the first component and -5 to 5 along the others. The bodies of device (o, d) lie in its own box of a recursive bisection of the volume: o picks a slab along the first component, and bit b of d halves the box along the second or third component; each block lies in its own sub-box of its device's box. `essential`: the 4 blocks of one device and level are distinct. `list_count`: A domain lists no pairs with its own outer index; some count equals 4 in every draw.
All inputs are finite; a program needn't handle non-finite values.
Results may differ from the reference program's by a relative error of at most 0.0003.
Values sent between devices are 32-bit elements; how exact they have to be, the bound alone decides.
No kernel may reach another device: no remote copies, remote signals or barrier semaphores. Data moves between devices by JAX's collectives and lax.ppermute only.
A program may use at most 64 MiB of HBM per device.

```python
import math
import jax
import jax.numpy as jnp
from jax import lax

BLOCK = 128
BLOCKS_DEV = 8
ESS_BLOCKS = 4
SLOTS = 4
LEVELS = 2
BODIES_DEV = 1024
BODIES = 32768
N_OUTER = 8
N_BISECT = 4
DEVICES = 32


def draw_positions(key, part):
    index = jnp.arange(BODIES, dtype=jnp.int32)
    device = index // BODIES_DEV
    outer_index = device // N_BISECT
    inner = device % N_BISECT
    block_index = index % BODIES_DEV // BLOCK
    cell_y = jnp.zeros_like(inner)
    cell_z = jnp.zeros_like(inner)
    for level in range(LEVELS):
        bit_value = inner // 2 ** level % 2
        if level % 2 == 0:
            cell_y = cell_y + bit_value * 2 ** (level // 2)
        else:
            cell_z = cell_z + bit_value * 2 ** (level // 2)
    count_y = 2 ** ((LEVELS + 1) // 2)
    count_z = 2 ** (LEVELS // 2)
    width_x = 0.5 / (N_OUTER * BLOCKS_DEV)
    width_y = 10.0 / count_y
    width_z = 10.0 / count_z
    low_x = -0.25 + (outer_index * BLOCKS_DEV + block_index).astype(jnp.float32) * width_x
    low_y = -5.0 + cell_y.astype(jnp.float32) * width_y
    low_z = -5.0 + cell_z.astype(jnp.float32) * width_z
    unit = jax.random.uniform(key, (3, BODIES), jnp.float32, 0.0, 1.0)
    along_x = unit[0]
    reach_y = unit[1] * unit[1] * unit[1]
    reach_z = unit[2] * unit[2] * unit[2]
    toward_y = cell_y * 2 < count_y
    toward_z = cell_z * 2 < count_z
    pos_x = low_x + width_x * along_x
    pos_y = jnp.where(toward_y, low_y + width_y * (1.0 - reach_y), low_y + width_y * reach_y)
    pos_z = jnp.where(toward_z, low_z + width_z * (1.0 - reach_z), low_z + width_z * reach_z)
    return jnp.stack([pos_x, pos_y, pos_z], axis=0).astype(jnp.float32)


def draw_essential(key, part):
    rows = DEVICES * LEVELS
    scores = jax.random.randint(key, (rows, BLOCKS_DEV), 0, 1 << 20) * BLOCKS_DEV + jnp.arange(BLOCKS_DEV, dtype=jnp.int32)[None, :]
    order = jnp.argsort(scores, axis=1)
    return order[:, :ESS_BLOCKS].astype(jnp.int32)


def draw_list_count(key, part):
    rows = N_OUTER * N_OUTER
    counts = jax.random.randint(key, (rows, N_BISECT), 0, SLOTS + 1)
    row_index = jnp.arange(rows, dtype=jnp.int32)[:, None]
    column = jnp.arange(N_BISECT, dtype=jnp.int32)[None, :]
    source_outer = row_index // N_OUTER
    target_outer = row_index % N_OUTER
    counts = jnp.where(((source_outer + 1) % N_OUTER == target_outer) & (column == 0), SLOTS, counts)
    counts = jnp.where(source_outer == target_outer, 0, counts)
    return counts.astype(jnp.int32)


def place_ends(values, stream_key, low, largest):
    spot = [jax.random.randint(jax.random.fold_in(stream_key, axis), (), 0, length) for axis, length in enumerate(values.shape)]
    longest = values.shape.index(max(values.shape))
    neighbour = spot[:longest] + [(spot[longest] + 1) % values.shape[longest]] + spot[longest + 1:]
    return values.at[tuple(spot)].set(low).at[tuple(neighbour)].set(largest)


def steps_of(key, extent, pieces, low, high):
    gain = 1.0
    for dim, shards_of in pieces:
        draws = jax.random.uniform(jax.random.fold_in(jax.random.fold_in(key, 6), dim), (shards_of,), jnp.float32, low / len(pieces), high / len(pieces))
        gain = gain * jnp.repeat(jnp.exp(draws), extent[dim] // shards_of).reshape((-1,) + (1,) * (len(extent) - 1 - dim))
    return gain


def scatter_about(own_key, shape, spread, most, pieces=(), held_as=jnp.bfloat16):
    factor_of = steps_of(own_key, shape, pieces, -0.22, 0.18) if pieces else 1.0
    array = jax.random.normal(own_key, shape, jnp.float32) * spread * factor_of
    return jnp.minimum(jnp.maximum(array, -most), most).astype(held_as)


def setup_inputs(seed: int = 0) -> dict:
    key_of = jax.random.split(jax.random.key(seed), 8)
    positions = draw_positions(jax.random.fold_in(key_of[7], 71), 0)
    masses = jnp.clip(jnp.exp(math.log(0.0078125) - 2.7725887 * jax.random.uniform(key_of[1], (BODIES,), jnp.float32) ** steps_of(key_of[1], (BODIES,), ((0, 32),), -0.2, 0.2)), 0.00048828125, 0.0078125)
    velocities = scatter_about(key_of[2], (3, BODIES), 0.5, 4.0, ((1, 32),), jnp.float32)
    essential = draw_essential(jax.random.fold_in(key_of[7], 71), 0)
    list_count = draw_list_count(jax.random.fold_in(key_of[7], 71), 0)
    list_target = place_ends(jax.random.randint(key_of[5], (N_OUTER * N_OUTER, N_BISECT, SLOTS), 0, BLOCKS_DEV), jax.random.fold_in(key_of[5], 1), 0, BLOCKS_DEV - 1).astype(jnp.int32)
    list_source = place_ends(jax.random.randint(key_of[6], (N_OUTER * N_OUTER, N_BISECT, SLOTS), 0, BLOCKS_DEV), jax.random.fold_in(key_of[6], 1), 0, BLOCKS_DEV - 1).astype(jnp.int32)
    return dict(positions=positions, masses=masses, velocities=velocities, essential=essential, list_count=list_count, list_target=list_target, list_source=list_source)


soften_sq = 0.01
time_step = 0.5

def pull(targets, sources):
    offset_x = sources[..., 0, None, :] - targets[..., 0, :, None]
    offset_y = sources[..., 1, None, :] - targets[..., 1, :, None]
    offset_z = sources[..., 2, None, :] - targets[..., 2, :, None]
    inverse = lax.rsqrt(offset_x * offset_x + offset_y * offset_y + offset_z * offset_z + soften_sq)
    weight = sources[..., 3, None, :] * inverse * inverse * inverse
    return jnp.stack([lax.optimization_barrier(jnp.sum(weight * offset_x, axis=-1)), lax.optimization_barrier(jnp.sum(weight * offset_y, axis=-1)), lax.optimization_barrier(jnp.sum(weight * offset_z, axis=-1))], axis=-2)

def essential_payload(blocks, chosen):
    picks = (chosen[:, None] == jnp.arange(blocks.shape[0], dtype=jnp.int32)[None, :]).astype(jnp.float32)
    whole = jnp.einsum('kn,nct->ckt', picks, blocks, precision=lax.Precision.HIGHEST).reshape(4, -1)
    totals = lax.optimization_barrier(jnp.sum(blocks[:, 3, :], axis=1))
    centre = lax.optimization_barrier(jnp.sum(blocks[:, :3, :] * blocks[:, 3:4, :], axis=2)) / totals[:, None]
    kept = totals * (1.0 - lax.optimization_barrier(jnp.sum(picks, axis=0)))
    monopole = jnp.concatenate([centre.T, kept[None, :]], axis=0)
    return (whole, monopole)

def reference(positions, masses, velocities, essential, list_count, list_target, list_source):
    with_mass = jnp.concatenate([positions, masses[None, :]], axis=0)
    per_device = with_mass.reshape(4, DEVICES, BODIES_DEV).transpose(1, 0, 2)
    all_blocks = per_device.reshape(DEVICES, 4, BLOCKS_DEV, BLOCK).transpose(0, 2, 1, 3)
    vel_dev = velocities.reshape(3, DEVICES, BODIES_DEV).transpose(1, 0, 2)
    chosen_all = essential.reshape(DEVICES, LEVELS, ESS_BLOCKS)
    counts = list_count.reshape(N_OUTER, N_OUTER, N_BISECT)
    target_ids = list_target.reshape(N_OUTER, N_OUTER, N_BISECT, SLOTS)
    source_ids = list_source.reshape(N_OUTER, N_OUTER, N_BISECT, SLOTS)

    def one_device(index):
        outer_index = index // N_BISECT
        inner = index % N_BISECT
        own = per_device[index]
        blocks = all_blocks[index]
        wholes = [own]
        monos = []
        for level in range(LEVELS):
            partner = outer_index * N_BISECT + jnp.bitwise_xor(inner, 1 << level)
            whole, mono = essential_payload(all_blocks[partner], chosen_all[partner, level])
            wholes.append(whole)
            monos.append(mono)
        near = pull(own[:3], jnp.concatenate(wholes, axis=1))
        far = pull(own[:3], jnp.concatenate(monos, axis=1))
        tids = target_ids[outer_index, :, inner, :]
        sids = source_ids[outer_index, :, inner, :]
        valid = (jnp.arange(SLOTS, dtype=jnp.int32)[None, :] < counts[outer_index, :, inner][:, None]).astype(jnp.float32)
        owners = jnp.arange(N_OUTER, dtype=jnp.int32) * N_BISECT + inner
        sources = all_blocks[owners[:, None], sids]
        targets = blocks[tids][:, :, :3, :]
        remote = pull(targets, sources) * valid[:, :, None, None]
        added = jnp.zeros((BLOCKS_DEV, 3, BLOCK), jnp.float32).at[tids].add(remote)
        added = added.transpose(1, 0, 2).reshape(3, BODIES_DEV)
        accel = near + far + added
        velocity = vel_dev[index] + time_step * accel
        position = own[:3] + time_step * velocity
        return (position, velocity)
    new_pos, new_vel = lax.map(one_device, jnp.arange(DEVICES, dtype=jnp.int32))
    return (new_pos.transpose(1, 0, 2).reshape(3, BODIES), new_vel.transpose(1, 0, 2).reshape(3, BODIES))
```

```python
import jax
import jax.numpy as jnp
from jax import lax
from jax.experimental import pallas as pl
from jax.experimental.pallas import tpu as pltpu
from jax.sharding import PartitionSpec as P

soften_sq = 0.01
time_step = 0.5
block = 128
f32 = jnp.float32
bf16 = jnp.bfloat16
vmem = pl.BlockSpec(memory_space=pltpu.VMEM)
smem = pl.BlockSpec(memory_space=pltpu.SMEM)


def exchange(value, axis, mask):
    pairs = [(source, source ^ mask) for source in range(lax.axis_size(axis))]
    return lax.ppermute(value, axis, pairs)


def split(value):
    high = value.astype(bf16).astype(f32)
    rest = value - high
    mid = rest.astype(bf16).astype(f32)
    return high, mid, rest - mid


def target_rows(points):
    high, mid, low = split(-2.0 * points[0:3])
    norm = jnp.sum(points[0:3] * points[0:3], axis=0, keepdims=True) + soften_sq
    one = jnp.ones_like(norm)
    return jnp.concatenate([high, mid, low, high, mid, high, one, one, one, *split(norm)], 0).astype(bf16)


def source_rows(points):
    high, mid, low = split(points[0:3])
    norm = jnp.sum(points[0:3] * points[0:3], axis=0, keepdims=True)
    one = jnp.ones_like(norm)
    return jnp.concatenate([high, high, high, mid, mid, low, *split(norm), one, one, one], 0).astype(bf16)


def moment_rows(points):
    moments = jnp.concatenate([points[0:3] * points[3:4], points[3:4]], 0)
    return jnp.concatenate([*split(moments), jnp.zeros_like(moments)], 0).astype(bf16)


def pull(columns, moments, targets):
    dist = jnp.dot(columns, targets, preferred_element_type=f32)
    inverse = lax.rsqrt(dist)
    weight = inverse * inverse * inverse
    high = weight.astype(bf16)
    low = (weight - high.astype(f32)).astype(bf16)
    return jnp.dot(moments, high, preferred_element_type=f32) + jnp.dot(
        moments, low, preferred_element_type=f32
    )


def flip(rows):
    return jnp.transpose(rows.astype(f32)).astype(bf16)


def pull_all(columns, moments, targets, step=256):
    parts = []
    for start in range(0, targets.shape[1], step):
        acc = None
        for first in range(0, columns.shape[0], step):
            part = pull(
                columns[first : first + step],
                moments[:, first : first + step],
                targets[:, start : start + step],
            )
            acc = part if acc is None else acc + part
        parts.append(acc)
    return jnp.concatenate(parts, 1)


def own_kernel(own_ref, out_ref):
    own = own_ref[:, : out_ref.shape[1]]
    out_ref[...] = pull_all(flip(source_rows(own)), moment_rows(own), target_rows(own))


def partner_kernel(picks, own_ref, other_ref, level, sums_ref, out_ref):
    bodies = out_ref.shape[1]
    count = bodies // block
    other = other_ref[:, :bodies]
    lane = lax.broadcasted_iota(jnp.int32, (1, block), 1)
    ids = other_ref[level : level + 1, bodies : bodies + block]
    power = jnp.zeros((1, block), f32)
    for pick in range(picks):
        power = jnp.where(lane == pick, float(count**pick), power)
    code = jnp.sum(ids * power).astype(jnp.int32)
    chosen = [(code // count**pick) % count for pick in range(picks)]
    moments = moment_rows(other)
    body = lax.broadcasted_iota(jnp.int32, (bodies, block), 0) // block
    place = lax.broadcasted_iota(jnp.int32, (bodies, block), 1)
    member = (body == place).astype(f32).astype(bf16)
    totals = jnp.dot(moments, member, preferred_element_type=f32)
    totals = totals[0:4] + totals[4:8] + totals[8:12]
    kept = lane < count
    for pick in chosen:
        kept = kept & (lane != pick)
    mass = jnp.where(lane < count, totals[3:4], 1.0)
    mono = jnp.concatenate([totals[0:3] / mass, jnp.where(kept, totals[3:4], 0.0)], 0)
    near = [other_ref[:, pl.ds(pl.multiple_of(pick * block, block), block)] for pick in chosen]
    points = jnp.concatenate(near + [mono], 1)
    whole = picks * block
    columns = flip(source_rows(points))
    moments = moment_rows(points)
    targets = target_rows(own_ref[:, :bodies])
    near = pull_all(columns[:whole], moments[:, :whole], targets)
    far = pull(columns[whole : whole + 16], moments[:, whole : whole + 16], targets)
    out_ref[...] = sums_ref[...] + near + far


def remote_kernel(here_ref, there_ref, count_ref, target_ref, source_ref, sums_ref, speed_ref,
                  position_ref, velocity_ref, rows_ref, acc_ref):
    bodies = sums_ref.shape[1]
    slots = target_ref.shape[1]
    place = lax.axis_index("outer")
    own = here_ref[0, :, :bodies]
    rows_ref[...] = target_rows(own)
    acc_ref[...] = sums_ref[...]
    half = here_ref.shape[0]

    def peer(group_ref, index, mask):
        other = place ^ mask
        points = []
        for slot in range(slots):
            start = pl.multiple_of(source_ref[other, slot] * block, block)
            points.append(group_ref[index, :, pl.ds(start, block)])
        points = jnp.concatenate(points, 1)
        columns = flip(source_rows(points))
        moments = moment_rows(points)
        for slot in range(slots):
            start = pl.multiple_of(target_ref[other, slot] * block, block)
            span = slice(slot * block, (slot + 1) * block)
            part = pull(columns[span], moments[:, span], rows_ref[:, pl.ds(start, block)])
            valid = jnp.where(slot < count_ref[other, 0], 1.0, 0.0)
            acc_ref[:, pl.ds(start, block)] += part * valid

    for index in range(1, half):
        peer(here_ref, index, 2 * index)
    for index in range(half):
        peer(there_ref, index, 2 * index + 1)
    total = acc_ref[0:4] + acc_ref[4:8] + acc_ref[8:12]
    position = own[0:3]
    velocity = speed_ref[...] + time_step * (total[0:3] - position * total[3:4])
    velocity_ref[...] = velocity
    position_ref[...] = position + time_step * velocity


def local(positions, masses, velocities, essential, list_count, list_target, list_source):
    bodies = positions.shape[1]
    levels = lax.axis_size("bisect").bit_length() - 1
    peers = lax.axis_size("outer")
    picks = essential.shape[1]
    slots = list_target.shape[2]
    sums = jax.ShapeDtypeStruct((16, bodies), f32)
    ids = jnp.pad(essential.astype(f32), ((0, 4 - levels), (0, block - picks)))
    own = jnp.concatenate([jnp.concatenate([positions, masses[None, :]], 0), ids], 1)
    across = [exchange(own, "bisect", 1 << level) for level in range(levels)]
    here = [own] + [exchange(own, "outer", mask) for mask in range(2, peers, 2)]
    here = jnp.stack(here)
    there = exchange(here, "outer", 1)
    acc = pl.pallas_call(own_kernel, out_shape=sums, in_specs=[vmem], out_specs=vmem)(own)
    for level in range(levels):
        acc = pl.pallas_call(
            lambda own_ref, other_ref, sums_ref, out_ref, level=level: partner_kernel(
                picks, own_ref, other_ref, level, sums_ref, out_ref
            ),
            out_shape=sums,
            in_specs=[vmem] * 3,
            out_specs=vmem,
        )(own, across[level], acc)
    shape = jax.ShapeDtypeStruct((3, bodies), f32)
    return pl.pallas_call(
        remote_kernel,
        out_shape=(shape, shape),
        in_specs=[vmem, vmem, smem, smem, smem, vmem, vmem],
        out_specs=(vmem, vmem),
        scratch_shapes=[pltpu.VMEM((24, bodies), bf16), pltpu.VMEM((16, bodies), f32)],
    )(here, there, list_count, list_target.reshape(peers, slots), list_source.reshape(peers, slots),
      acc, velocities)


def solution(mesh):
    placed = (
        P(None, ("outer", "bisect")),
        P(("outer", "bisect")),
        P(None, ("outer", "bisect")),
        P(("outer", "bisect"), None),
        P("outer", "bisect"),
        P("outer", "bisect", None),
        P("outer", "bisect", None),
    )
    return jax.shard_map(
        local,
        mesh=mesh,
        in_specs=placed,
        out_specs=(P(None, ("outer", "bisect")), P(None, ("outer", "bisect"))),
        check_vma=False,
    )
```

```python
import jax
import jax.numpy as jnp
from jax import lax
from jax.experimental import pallas as pl
from jax.experimental.pallas import tpu as pltpu
from jax.sharding import PartitionSpec as P


soften_sq = 0.01
time_step = 0.5
block = 128
f32 = jnp.float32
bf16 = jnp.bfloat16
vmem = pl.BlockSpec(memory_space=pltpu.VMEM)
smem = pl.BlockSpec(memory_space=pltpu.SMEM)


def exchange(value, axis, mask):
    pairs = [(source, source ^ mask) for source in range(lax.axis_size(axis))]
    return lax.ppermute(value, axis, pairs)


def split(value):
    high = value.astype(bf16).astype(f32)
    rest = value - high
    mid = rest.astype(bf16).astype(f32)
    return high, mid, rest - mid


def target_rows(points):
    high, mid, low = split(-2.0 * points[0:3])
    norm = jnp.sum(points[0:3] * points[0:3], axis=0, keepdims=True) + soften_sq
    one = jnp.ones_like(norm)
    return jnp.concatenate([high, mid, low, high, mid, high, one, one, one, *split(norm)], 0).astype(bf16)


def source_rows(points):
    high, mid, low = split(points[0:3])
    norm = jnp.sum(points[0:3] * points[0:3], axis=0, keepdims=True)
    one = jnp.ones_like(norm)
    return jnp.concatenate([high, high, high, mid, mid, low, *split(norm), one, one, one], 0).astype(bf16)


def moment_rows(points):
    moments = jnp.concatenate([points[0:3] * points[3:4], points[3:4]], 0)
    return jnp.concatenate([*split(moments), jnp.zeros_like(moments)], 0).astype(bf16)


def pull(columns, moments, targets):
    dist = jnp.dot(columns, targets, preferred_element_type=f32)
    inverse = lax.rsqrt(dist)
    weight = inverse * inverse * inverse
    high = weight.astype(bf16)
    low = (weight - high.astype(f32)).astype(bf16)
    return jnp.dot(moments, high, preferred_element_type=f32) + jnp.dot(
        moments, low, preferred_element_type=f32
    )


def flip(rows):
    return jnp.transpose(rows.astype(f32)).astype(bf16)


def pull_all(columns, moments, targets, step=256):
    parts = []
    for start in range(0, targets.shape[1], step):
        acc = None
        for first in range(0, columns.shape[0], step):
            part = pull(
                columns[first : first + step],
                moments[:, first : first + step],
                targets[:, start : start + step],
            )
            acc = part if acc is None else acc + part
        parts.append(acc)
    return jnp.concatenate(parts, 1)


def kept(value):
    return pltpu.with_memory_space_constraint(value, pltpu.VMEM)


def pack_kernel(essential_ref, position_ref, mass_ref, own_ref):
    levels, picks = essential_ref.shape
    bodies = position_ref.shape[1]
    count = bodies // block
    own_ref[0:3, :bodies] = position_ref[...]
    own_ref[3:4, :bodies] = mass_ref[...]
    row = lax.broadcasted_iota(jnp.int32, (4, block), 0)
    codes = jnp.zeros((4, block), f32)
    for level in range(levels):
        code = 0
        for pick in range(picks):
            code = code * count + essential_ref[level, pick]
        codes = jnp.where(row == level, code.astype(f32), codes)
    own_ref[:, bodies:] = codes


def own_kernel(own_ref, out_ref):
    own = own_ref[:, : out_ref.shape[1]]
    out_ref[...] = pull_all(flip(source_rows(own)), moment_rows(own), target_rows(own))


def partner_kernel(picks, own_ref, other_ref, level, sums_ref, out_ref):
    bodies = out_ref.shape[1]
    count = bodies // block
    other = other_ref[:, :bodies]
    lane = lax.broadcasted_iota(jnp.int32, (1, block), 1)
    code = jnp.max(other_ref[level : level + 1, bodies : bodies + block]).astype(jnp.int32)
    chosen = [(code // count**pick) % count for pick in range(picks)]
    moments = moment_rows(other)
    body = lax.broadcasted_iota(jnp.int32, (bodies, block), 0) // block
    place = lax.broadcasted_iota(jnp.int32, (bodies, block), 1)
    member = (body == place).astype(f32).astype(bf16)
    totals = jnp.dot(moments, member, preferred_element_type=f32)
    totals = totals[0:4] + totals[4:8] + totals[8:12]
    kept = lane < count
    for pick in chosen:
        kept = kept & (lane != pick)
    mass = jnp.where(lane < count, totals[3:4], 1.0)
    mono = jnp.concatenate([totals[0:3] / mass, jnp.where(kept, totals[3:4], 0.0)], 0)
    near = [other_ref[:, pl.ds(pl.multiple_of(pick * block, block), block)] for pick in chosen]
    points = jnp.concatenate(near + [mono], 1)
    whole = picks * block
    columns = flip(source_rows(points))
    moments = moment_rows(points)
    targets = target_rows(own_ref[:, :bodies])
    near = pull_all(columns[:whole], moments[:, :whole], targets)
    far = pull(columns[whole : whole + 16], moments[:, whole : whole + 16], targets)
    out_ref[...] = sums_ref[...] + near + far


def remote_kernel(here_ref, there_ref, count_ref, target_ref, source_ref, sums_ref, speed_ref,
                  position_ref, velocity_ref, rows_ref, acc_ref):
    bodies = sums_ref.shape[1]
    slots = target_ref.shape[0]
    place = lax.axis_index("outer")
    own = here_ref[0, :, :bodies]
    rows_ref[...] = target_rows(own)
    acc_ref[...] = sums_ref[...]
    half = here_ref.shape[0]

    def peer(group_ref, index, mask):
        other = place ^ mask
        points = []
        for slot in range(slots):
            start = pl.multiple_of(source_ref[slot, other] * block, block)
            points.append(group_ref[index, :, pl.ds(start, block)])
        points = jnp.concatenate(points, 1)
        columns = flip(source_rows(points))
        moments = moment_rows(points)
        for slot in range(slots):
            start = pl.multiple_of(target_ref[slot, other] * block, block)
            span = slice(slot * block, (slot + 1) * block)
            part = pull(columns[span], moments[:, span], rows_ref[:, pl.ds(start, block)])
            valid = jnp.where(slot < count_ref[0, other], 1.0, 0.0)
            acc_ref[:, pl.ds(start, block)] += part * valid

    for index in range(1, half):
        peer(here_ref, index, 2 * index)
    for index in range(half):
        peer(there_ref, index, 2 * index + 1)
    total = acc_ref[0:4] + acc_ref[4:8] + acc_ref[8:12]
    position = own[0:3]
    velocity = speed_ref[...] + time_step * (total[0:3] - position * total[3:4])
    velocity_ref[...] = velocity
    position_ref[...] = position + time_step * velocity


def local(positions, masses, velocities, essential, list_count, list_target, list_source):
    bodies = positions.shape[1]
    levels = lax.axis_size("bisect").bit_length() - 1
    peers = lax.axis_size("outer")
    picks = essential.shape[1]
    slots = list_target.shape[2]
    sums = pltpu.VMEM((16, bodies), f32)
    own = pl.pallas_call(
        pack_kernel,
        out_shape=pltpu.VMEM((4, bodies + block), f32),
        in_specs=[smem, vmem, vmem],
        out_specs=vmem,
    )(essential, positions, masses.reshape(1, bodies))
    across = []
    for level in range(levels):
        across.append(exchange(own, "bisect", 1 << level))
    here = [own]
    for mask in range(2, peers, 2):
        here.append(exchange(own, "outer", mask))
    here = jnp.stack(here)
    there = exchange(here, "outer", 1)
    acc = pl.pallas_call(own_kernel, out_shape=sums, in_specs=[vmem], out_specs=vmem)(kept(own))
    for level in range(levels):
        acc = pl.pallas_call(
            lambda own_ref, other_ref, sums_ref, out_ref, level=level: partner_kernel(
                picks, own_ref, other_ref, level, sums_ref, out_ref
            ),
            out_shape=sums,
            in_specs=[vmem] * 3,
            out_specs=vmem,
        )(kept(own), kept(across[level]), kept(acc))
    shape = jax.ShapeDtypeStruct((3, bodies), f32)
    return pl.pallas_call(
        remote_kernel,
        out_shape=(shape, shape),
        in_specs=[vmem, vmem, smem, smem, smem, vmem, vmem],
        out_specs=(vmem, vmem),
        scratch_shapes=[pltpu.VMEM((24, bodies), bf16), pltpu.VMEM((16, bodies), f32)],
    )(
        kept(here),
        kept(there),
        list_count.T,
        list_target.reshape(peers, slots).T,
        list_source.reshape(peers, slots).T,
        kept(acc),
        velocities,
    )


def solution(mesh):
    placed = (
        P(None, ("outer", "bisect")),
        P(("outer", "bisect")),
        P(None, ("outer", "bisect")),
        P(("outer", "bisect"), None),
        P("outer", "bisect"),
        P("outer", "bisect", None),
        P("outer", "bisect", None),
    )
    return jax.shard_map(
        local,
        mesh=mesh,
        in_specs=placed,
        out_specs=(P(None, ("outer", "bisect")), P(None, ("outer", "bisect"))),
        check_vma=False,
    )
```

```python
import functools

import jax
import jax.numpy as jnp
from jax import lax
from jax.experimental import pallas as pl
from jax.experimental.pallas import tpu as pltpu
from jax.sharding import PartitionSpec as P


soften_sq = 0.01
time_step = 0.5
block = 128
cells = 32.0
mark = 2.0**-7
f32 = jnp.float32
bf16 = jnp.bfloat16
vmem = pl.BlockSpec(memory_space=pltpu.VMEM)
smem = pl.BlockSpec(memory_space=pltpu.SMEM)
hbm = pl.BlockSpec(memory_space=pl.ANY)


def exchange(value, axis, mask):
    pairs = [(source, source ^ mask) for source in range(lax.axis_size(axis))]
    return lax.ppermute(value, axis, pairs)


def rounded(value):
    return value.astype(bf16).astype(f32)


def split(value):
    high = rounded(value)
    rest = value - high
    mid = rounded(rest)
    return high, mid, rest - mid


def on_grid(points):
    row = lax.broadcasted_iota(jnp.int32, points.shape, 0)
    points = jnp.where(row == 3, 1.0 + mark, points)
    grid = jnp.round(points * cells) * (1.0 / cells)
    rest = points - grid
    high = rounded(rest)
    norm = jnp.sum((grid * grid)[0:3], axis=0, keepdims=True)
    coarse = rounded(norm)
    fine = (norm - coarse) + jnp.sum(((2.0 * grid + rest) * rest)[0:3], axis=0, keepdims=True)
    return grid, high, rest - high, coarse, fine


def target_rows(points):
    grid, high, low, coarse, fine = on_grid(points)
    grid, high, low = -2.0 * grid[0:3], -2.0 * high[0:3], -2.0 * low[0:3]
    first, second, third = split(fine + soften_sq)
    one, zero = jnp.ones_like(fine), jnp.zeros_like(fine)
    return jnp.concatenate(
        [grid, coarse, one, one, one, one, high, first, low, second]
        + [grid, third * (1.0 / mark), grid, zero, high, zero, low, zero],
        0,
    ).astype(bf16)


def source_rows(points):
    grid, high, low, coarse, fine = on_grid(points)
    scalars = jnp.concatenate([coarse, *split(fine)], 0)
    return jnp.concatenate([grid, scalars, grid, grid, high, low, high, high], 0).astype(bf16)


def moment_rows(points):
    row = lax.broadcasted_iota(jnp.int32, points.shape, 0)
    moments = jnp.where(row == 3, 1.0, points) * points[3:4]
    return jnp.concatenate([*split(moments), jnp.zeros_like(moments)], 0).astype(bf16)


def pull(columns, moments, targets):
    dist = jnp.dot(columns, targets, preferred_element_type=f32)
    inverse = lax.rsqrt(dist)
    weight = inverse * inverse * inverse
    high = weight.astype(bf16)
    low = (weight - high.astype(f32)).astype(bf16)
    return jnp.dot(moments, high, preferred_element_type=f32) + jnp.dot(
        moments, low, preferred_element_type=f32
    )


def flip(rows):
    return jnp.transpose(rows.astype(f32)).astype(bf16)


def pull_all(columns, moments, targets, step=256):
    parts = []
    for start in range(0, targets.shape[1], step):
        acc = None
        for first in range(0, columns.shape[0], step):
            part = pull(
                columns[first : first + step],
                moments[:, first : first + step],
                targets[:, start : start + step],
            )
            acc = part if acc is None else acc + part
        parts.append(acc)
    return jnp.concatenate(parts, 1)


def kept(value):
    return pltpu.with_memory_space_constraint(value, pltpu.VMEM)


def pack_kernel(essential_ref, position_ref, mass_ref, own_ref):
    levels, picks = essential_ref.shape
    bodies = position_ref.shape[1]
    count = bodies // block
    own_ref[0:3, :bodies] = position_ref[...]
    own_ref[3:4, :bodies] = mass_ref[...]
    row = lax.broadcasted_iota(jnp.int32, (4, block), 0)
    codes = jnp.zeros((4, block), f32)
    for level in range(levels):
        code = 0
        for pick in range(picks):
            code = code * count + essential_ref[level, pick]
        codes = jnp.where(row == level, code.astype(f32), codes)
    own_ref[:, bodies:] = codes


def own_kernel(own_ref, rows_ref, out_ref):
    own = own_ref[:, : out_ref.shape[1]]
    rows = target_rows(own)
    rows_ref[...] = rows
    out_ref[...] = pull_all(flip(source_rows(own)), moment_rows(own), rows)


def partner_pulls(picks, level, other_ref, rows_ref):
    bodies = rows_ref.shape[1]
    count = bodies // block
    other = other_ref[:, :bodies]
    lane = lax.broadcasted_iota(jnp.int32, (1, block), 1)
    code = jnp.max(other_ref[level : level + 1, bodies : bodies + block]).astype(jnp.int32)
    chosen = [(code // count**pick) % count for pick in range(picks)]
    moments = moment_rows(other)
    body = lax.broadcasted_iota(jnp.int32, (bodies, block), 0) // block
    place = lax.broadcasted_iota(jnp.int32, (bodies, block), 1)
    member = (body == place).astype(f32).astype(bf16)
    totals = jnp.dot(moments, member, preferred_element_type=f32)
    totals = totals[0:4] + totals[4:8] + totals[8:12]
    kept = lane < count
    for pick in chosen:
        kept = kept & (lane != pick)
    mass = jnp.where(lane < count, totals[3:4], 1.0)
    mono = jnp.concatenate([totals[0:3] / mass, jnp.where(kept, totals[3:4], 0.0)], 0)
    near = [other_ref[:, pl.ds(pl.multiple_of(pick * block, block), block)] for pick in chosen]
    points = jnp.concatenate(near + [mono], 1)
    whole = picks * block
    last = whole + (count + 15) // 16 * 16
    columns = flip(source_rows(points))
    moments = moment_rows(points)
    rows = rows_ref[...]
    near = pull_all(columns[:whole], moments[:, :whole], rows)
    return near + pull(columns[whole:last], moments[:, whole:last], rows)


def partner_kernel(picks, level, rows_ref, other_ref, sums_ref, out_ref):
    out_ref[...] = sums_ref[...] + partner_pulls(picks, level, other_ref, rows_ref)


def remote_kernel(picks, level, rows_ref, other_ref, here_ref, there_ref, sums_ref, speed_ref,
                  counts_ref, targets_ref, sources_ref, position_ref, velocity_ref,
                  acc_ref, count_ref, target_ref, source_ref, done_ref):
    lists = [
        pltpu.make_async_copy(far, near, done_ref.at[index])
        for index, (far, near) in enumerate(
            [(counts_ref, count_ref), (targets_ref, target_ref), (sources_ref, source_ref)]
        )
    ]
    for copy in lists:
        copy.start()
    bodies = sums_ref.shape[1]
    slots = target_ref.shape[0]
    place = lax.axis_index("outer")
    half = here_ref.shape[0]
    acc_ref[...] = sums_ref[...] + partner_pulls(picks, level, other_ref, rows_ref)
    for copy in lists:
        copy.wait()

    def peer(group_ref, index, mask):
        other = place ^ mask
        points = []
        for slot in range(slots):
            start = pl.multiple_of(source_ref[slot, other] * block, block)
            points.append(group_ref[index, :, pl.ds(start, block)])
        points = jnp.concatenate(points, 1)
        columns = flip(source_rows(points))
        moments = moment_rows(points)
        for slot in range(slots):
            start = pl.multiple_of(target_ref[slot, other] * block, block)
            span = slice(slot * block, (slot + 1) * block)
            part = pull(columns[span], moments[:, span], rows_ref[:, pl.ds(start, block)])
            valid = jnp.where(slot < count_ref[0, other], 1.0, 0.0)
            acc_ref[:, pl.ds(start, block)] += part * valid

    for index in range(1, half):
        peer(here_ref, index, 2 * index)
    for index in range(half):
        peer(there_ref, index, 2 * index + 1)
    total = acc_ref[0:4] + acc_ref[4:8] + acc_ref[8:12]
    position = here_ref[0, 0:3, :bodies]
    velocity = speed_ref[...] + time_step * (total[0:3] - position * total[3:4])
    velocity_ref[...] = velocity
    position_ref[...] = position + time_step * velocity


def local(positions, masses, velocities, essential, list_count, list_target, list_source):
    bodies = positions.shape[1]
    levels = lax.axis_size("bisect").bit_length() - 1
    peers = lax.axis_size("outer")
    picks = essential.shape[1]
    slots = list_target.shape[2]
    sums = pltpu.VMEM((16, bodies), f32)
    own = pl.pallas_call(
        pack_kernel,
        out_shape=pltpu.VMEM((4, bodies + block), f32),
        in_specs=[smem, vmem, vmem],
        out_specs=vmem,
    )(essential, positions, masses.reshape(1, bodies))
    across = []
    for level in range(levels):
        across.append(exchange(own, "bisect", 1 << level))
    here = [own]
    for mask in range(2, peers, 2):
        here.append(exchange(own, "outer", mask))
    here = jnp.stack(here)
    there = exchange(here, "outer", 1)
    rows, acc = pl.pallas_call(
        own_kernel,
        out_shape=(pltpu.VMEM((32, bodies), bf16), sums),
        in_specs=[vmem],
        out_specs=(vmem, vmem),
    )(kept(own))
    for level in range(levels - 1):
        acc = pl.pallas_call(
            functools.partial(partner_kernel, picks, level),
            out_shape=sums,
            in_specs=[vmem] * 3,
            out_specs=vmem,
        )(kept(rows), kept(across[level]), kept(acc))
    shape = jax.ShapeDtypeStruct((3, bodies), f32)
    return pl.pallas_call(
        functools.partial(remote_kernel, picks, levels - 1),
        out_shape=(shape, shape),
        in_specs=[vmem] * 6 + [hbm] * 3,
        out_specs=(vmem, vmem),
        scratch_shapes=[
            pltpu.VMEM((16, bodies), f32),
            pltpu.SMEM((1, peers), jnp.int32),
            pltpu.SMEM((slots, peers), jnp.int32),
            pltpu.SMEM((slots, peers), jnp.int32),
            pltpu.SemaphoreType.DMA((3,)),
        ],
    )(
        kept(rows),
        kept(across[levels - 1]),
        kept(here),
        kept(there),
        kept(acc),
        kept(velocities),
        list_count.T,
        list_target.reshape(peers, slots).T,
        list_source.reshape(peers, slots).T,
    )


def solution(mesh):
    placed = (
        P(None, ("outer", "bisect")),
        P(("outer", "bisect")),
        P(None, ("outer", "bisect")),
        P(("outer", "bisect"), None),
        P("outer", "bisect"),
        P("outer", "bisect", None),
        P("outer", "bisect", None),
    )
    return jax.shard_map(
        local,
        mesh=mesh,
        in_specs=placed,
        out_specs=(P(None, ("outer", "bisect")), P(None, ("outer", "bisect"))),
        check_vma=False,
    )
```

```python
import functools

import jax
import jax.numpy as jnp
from jax import lax
from jax.experimental import pallas as pl
from jax.experimental.pallas import tpu as pltpu
from jax.sharding import PartitionSpec as P


soften_sq = 0.01
time_step = 0.5
block = 128
cells = 32.0
mark = 2.0**-7
f32 = jnp.float32
bf16 = jnp.bfloat16
vmem = pl.BlockSpec(memory_space=pltpu.VMEM)
smem = pl.BlockSpec(memory_space=pltpu.SMEM)
hbm = pl.BlockSpec(memory_space=pl.ANY)


def exchange(value, axis, mask):
    pairs = [(source, source ^ mask) for source in range(lax.axis_size(axis))]
    return lax.ppermute(value, axis, pairs)


def rounded(value):
    return value.astype(bf16).astype(f32)


def split(value):
    high = rounded(value)
    rest = value - high
    mid = rounded(rest)
    return high, mid, rest - mid


def on_grid(points):
    row = lax.broadcasted_iota(jnp.int32, points.shape, 0)
    points = jnp.where(row == 3, 1.0 + mark, points)
    grid = jnp.round(points * cells) * (1.0 / cells)
    rest = points - grid
    high = rounded(rest)
    norm = jnp.sum((grid * grid)[0:3], axis=0, keepdims=True)
    coarse = rounded(norm)
    fine = (norm - coarse) + jnp.sum(((2.0 * grid + rest) * rest)[0:3], axis=0, keepdims=True)
    return grid, high, rest - high, coarse, fine


def target_rows(points):
    grid, high, low, coarse, fine = on_grid(points)
    grid, high, low = -2.0 * grid[0:3], -2.0 * high[0:3], -2.0 * low[0:3]
    first, second, third = split(fine + soften_sq)
    one, zero = jnp.ones_like(fine), jnp.zeros_like(fine)
    return jnp.concatenate(
        [grid, coarse, one, one, one, one, high, first, low, second]
        + [grid, third * (1.0 / mark), grid, zero, high, zero, low, zero],
        0,
    ).astype(bf16)


def source_rows(points):
    grid, high, low, coarse, fine = on_grid(points)
    scalars = jnp.concatenate([coarse, *split(fine)], 0)
    return jnp.concatenate([grid, scalars, grid, grid, high, low, high, high], 0).astype(bf16)


def moment_rows(points):
    row = lax.broadcasted_iota(jnp.int32, points.shape, 0)
    moments = jnp.where(row == 3, 1.0, points) * points[3:4]
    return jnp.concatenate([*split(moments), jnp.zeros_like(moments)], 0).astype(bf16)


def distances(columns, targets):
    return jnp.dot(columns, targets, preferred_element_type=f32)


def weighted(moments, dist):
    inverse = lax.rsqrt(dist)
    weight = inverse * inverse * inverse
    high = weight.astype(bf16)
    low = (weight - high.astype(f32)).astype(bf16)
    return jnp.dot(moments, high, preferred_element_type=f32) + jnp.dot(
        moments, low, preferred_element_type=f32
    )


def staged(tasks, depth):
    waiting = []
    for start, finish in tasks:
        waiting.append((start(), finish))
        if len(waiting) > depth:
            dist, done = waiting.pop(0)
            done(dist)
    for dist, done in waiting:
        done(dist)


def flip(rows):
    return jnp.transpose(rows.astype(f32)).astype(bf16)


def pull_tasks(columns, moments, targets, store, tile=256, step=256):
    def task(start, first, last):
        def begin():
            return distances(columns[first:last], targets[:, start : start + tile])

        def end(dist):
            store(start, weighted(moments[:, first:last], dist))

        return begin, end

    total = columns.shape[0]
    return [
        task(start, first, min(first + step, total))
        for start in range(0, targets.shape[1], tile)
        for first in range(0, total, step)
    ]


def pull_all(columns, moments, targets, depth):
    parts = {}

    def store(start, part):
        parts[start] = parts[start] + part if start in parts else part

    staged(pull_tasks(columns, moments, targets, store), depth)
    return jnp.concatenate([parts[start] for start in sorted(parts)], 1)


def kept(value):
    return pltpu.with_memory_space_constraint(value, pltpu.VMEM)


def pack_kernel(essential_ref, position_ref, mass_ref, own_ref):
    levels, picks = essential_ref.shape
    bodies = position_ref.shape[1]
    count = bodies // block
    own_ref[0:3, :bodies] = position_ref[...]
    own_ref[3:4, :bodies] = mass_ref[...]
    row = lax.broadcasted_iota(jnp.int32, (4, block), 0)
    codes = jnp.zeros((4, block), f32)
    for level in range(levels):
        code = 0
        for pick in range(picks):
            code = code * count + essential_ref[level, pick]
        codes = jnp.where(row == level, code.astype(f32), codes)
    own_ref[:, bodies:] = codes


def own_kernel(own_ref, rows_ref, out_ref):
    own = own_ref[:, : out_ref.shape[1]]
    rows = target_rows(own)
    rows_ref[...] = rows
    out_ref[...] = pull_all(flip(source_rows(own)), moment_rows(own), rows, 1)


def partner_pulls(picks, level, other_ref, rows_ref):
    bodies = rows_ref.shape[1]
    count = bodies // block
    other = other_ref[:, :bodies]
    lane = lax.broadcasted_iota(jnp.int32, (1, block), 1)
    code = jnp.max(other_ref[level : level + 1, bodies : bodies + block]).astype(jnp.int32)
    chosen = [(code // count**pick) % count for pick in range(picks)]
    moments = moment_rows(other)
    body = lax.broadcasted_iota(jnp.int32, (bodies, block), 0) // block
    place = lax.broadcasted_iota(jnp.int32, (bodies, block), 1)
    member = (body == place).astype(f32).astype(bf16)
    totals = jnp.dot(moments, member, preferred_element_type=f32)
    totals = totals[0:4] + totals[4:8] + totals[8:12]
    kept = lane < count
    for pick in chosen:
        kept = kept & (lane != pick)
    mass = jnp.where(lane < count, totals[3:4], 1.0)
    mono = jnp.concatenate([totals[0:3] / mass, jnp.where(kept, totals[3:4], 0.0)], 0)
    near = [other_ref[:, pl.ds(pl.multiple_of(pick * block, block), block)] for pick in chosen]
    points = jnp.concatenate(near + [mono], 1)
    whole = picks * block
    last = whole + (count + 15) // 16 * 16
    columns = flip(source_rows(points))
    moments = moment_rows(points)
    rows = rows_ref[...]
    near = pull_all(columns[:whole], moments[:, :whole], rows, 2)
    far = weighted(moments[:, whole:last], distances(columns[whole:last], rows))
    return near + far


def partner_kernel(picks, level, rows_ref, other_ref, sums_ref, out_ref):
    out_ref[...] = sums_ref[...] + partner_pulls(picks, level, other_ref, rows_ref)


def remote_kernel(picks, level, rows_ref, other_ref, here_ref, there_ref, sums_ref, speed_ref,
                  counts_ref, targets_ref, sources_ref, position_ref, velocity_ref,
                  acc_ref, count_ref, target_ref, source_ref, done_ref):
    lists = [
        pltpu.make_async_copy(far, near, done_ref.at[index])
        for index, (far, near) in enumerate(
            [(counts_ref, count_ref), (targets_ref, target_ref), (sources_ref, source_ref)]
        )
    ]
    for copy in lists:
        copy.start()
    bodies = sums_ref.shape[1]
    slots = target_ref.shape[0]
    place = lax.axis_index("outer")
    half = here_ref.shape[0]
    acc_ref[...] = sums_ref[...] + partner_pulls(picks, level, other_ref, rows_ref)
    for copy in lists:
        copy.wait()

    def peer(group_ref, index, mask):
        other = place ^ mask
        points = []
        for slot in range(slots):
            start = pl.multiple_of(source_ref[slot, other] * block, block)
            points.append(group_ref[index, :, pl.ds(start, block)])
        points = jnp.concatenate(points, 1)
        columns = flip(source_rows(points))
        moments = moment_rows(points)

        def task(slot):
            start = pl.multiple_of(target_ref[slot, other] * block, block)
            span = slice(slot * block, (slot + 1) * block)

            def begin():
                return distances(columns[span], rows_ref[:, pl.ds(start, block)])

            def end(dist):
                valid = jnp.where(slot < count_ref[0, other], 1.0, 0.0)
                acc_ref[:, pl.ds(start, block)] += weighted(moments[:, span], dist) * valid

            return begin, end

        return [task(slot) for slot in range(slots)]

    peers = [(here_ref, index, 2 * index) for index in range(1, half)]
    peers += [(there_ref, index, 2 * index + 1) for index in range(half)]
    staged((task for item in peers for task in peer(*item)), 8)
    total = acc_ref[0:4] + acc_ref[4:8] + acc_ref[8:12]
    position = here_ref[0, 0:3, :bodies]
    velocity = speed_ref[...] + time_step * (total[0:3] - position * total[3:4])
    velocity_ref[...] = velocity
    position_ref[...] = position + time_step * velocity


def local(positions, masses, velocities, essential, list_count, list_target, list_source):
    bodies = positions.shape[1]
    levels = lax.axis_size("bisect").bit_length() - 1
    peers = lax.axis_size("outer")
    picks = essential.shape[1]
    slots = list_target.shape[2]
    sums = pltpu.VMEM((16, bodies), f32)
    own = pl.pallas_call(
        pack_kernel,
        out_shape=pltpu.VMEM((4, bodies + block), f32),
        in_specs=[smem, vmem, vmem],
        out_specs=vmem,
    )(essential, positions, masses.reshape(1, bodies))
    across = []
    for level in range(levels):
        across.append(exchange(own, "bisect", 1 << level))
    here = [own]
    for mask in range(2, peers, 2):
        here.append(exchange(own, "outer", mask))
    here = jnp.stack(here)
    there = exchange(here, "outer", 1)
    rows, acc = pl.pallas_call(
        own_kernel,
        out_shape=(pltpu.VMEM((32, bodies), bf16), sums),
        in_specs=[vmem],
        out_specs=(vmem, vmem),
    )(kept(own))
    for level in range(levels - 1):
        acc = pl.pallas_call(
            functools.partial(partner_kernel, picks, level),
            out_shape=sums,
            in_specs=[vmem] * 3,
            out_specs=vmem,
        )(kept(rows), kept(across[level]), kept(acc))
    shape = jax.ShapeDtypeStruct((3, bodies), f32)
    return pl.pallas_call(
        functools.partial(remote_kernel, picks, levels - 1),
        out_shape=(shape, shape),
        in_specs=[vmem] * 6 + [hbm] * 3,
        out_specs=(vmem, vmem),
        scratch_shapes=[
            pltpu.VMEM((16, bodies), f32),
            pltpu.SMEM((1, peers), jnp.int32),
            pltpu.SMEM((slots, peers), jnp.int32),
            pltpu.SMEM((slots, peers), jnp.int32),
            pltpu.SemaphoreType.DMA((3,)),
        ],
    )(
        kept(rows),
        kept(across[levels - 1]),
        kept(here),
        kept(there),
        kept(acc),
        kept(velocities),
        list_count.T,
        list_target.reshape(peers, slots).T,
        list_source.reshape(peers, slots).T,
    )


def solution(mesh):
    placed = (
        P(None, ("outer", "bisect")),
        P(("outer", "bisect")),
        P(None, ("outer", "bisect")),
        P(("outer", "bisect"), None),
        P("outer", "bisect"),
        P("outer", "bisect", None),
        P("outer", "bisect", None),
    )
    return jax.shard_map(
        local,
        mesh=mesh,
        in_specs=placed,
        out_specs=(P(None, ("outer", "bisect")), P(None, ("outer", "bisect"))),
        check_vma=False,
    )
```
